512 devices in a mesh: span: 64 (over z, x), seq: 8 (over y, core).
Axes of the slice: x: 4, y: 4, z: 16, core: 2. Of those that a mesh axis runs over, the one named last changes fastest.
Arguments:
- queries: bfloat16 [65536, 3072], P(('span', 'seq')), may hold values from -64 to 64
- keys: bfloat16 [65536, 3072], P(('span', 'seq')), may hold values from -4 to 4
- values: bfloat16 [65536, 3072], P(('span', 'seq')), may hold values from -6 to 6
- latent: bfloat16 [65536, 3072], P(('span', 'seq')), may hold values from -6 to 6
- fresh_noise: bfloat16 [1024, 3072], P('seq'), may hold values from -6 to 6
- pool_weight: bfloat16 [32, 24], replicated, may hold values from -1 to 1
- gate_table: bfloat16 [64, 3072], replicated, may hold values from -4 to 4
- levels: int32 [64], P('span'), may hold values from 0 to 63
Outputs:
- next_latent: bfloat16 [65536, 3072], P(('span', 'seq'))
The draws below stay inside these ranges and needn't reach their ends.
All inputs are finite; a program needn't handle non-finite values.
Results may differ from the reference program's by a relative error of at most 0.005.
Values may be sent and summed in bfloat16 or wider, within the bound.
A program may use at most 64 MiB of HBM per device.

```python
import jax
import jax.numpy as jnp
from jax import lax

HEADS = 24
HEAD_DIM = 128
POOL = 32
LEVELS = 64
CHANNELS = 3072
SPAN_TOK = 1024
TOKENS = 65536
N_SPAN = 64


def draw_pair(key):
    base = jax.random.fold_in(key, 7001)
    key_query, key_key = jax.random.split(base, 2)
    query_draw = jnp.clip(jax.random.normal(key_query, (TOKENS, CHANNELS), jnp.float32), -4.0, 4.0)
    key_draw = jnp.clip(jax.random.normal(key_key, (TOKENS, CHANNELS), jnp.float32), -4.0, 4.0)
    return (query_draw, key_draw)


def draw_queries(key, part):
    return draw_pair(key)[0].astype(jnp.bfloat16)


def draw_keys(key, part):
    return draw_pair(key)[1].astype(jnp.bfloat16)


def place_ends(array, rng, low, top_value):
    shape = array.shape
    index_at = [jax.random.randint(jax.random.fold_in(rng, axis), (), 0, shape[axis]) for axis in range(len(shape))]
    array = array.at[tuple(index_at)].set(low)
    longest = shape.index(max(shape))
    index_at[longest] = (index_at[longest] + 1) % shape[longest]
    return array.at[tuple(index_at)].set(top_value)


def block_levels(key, extent, cuts, least, largest):
    level = 1.0
    for dim, shards_of in cuts:
        steps = jax.random.uniform(jax.random.fold_in(jax.random.fold_in(key, 6), dim), (shards_of,), jnp.float32, least / len(cuts), largest / len(cuts))
        level = level * jnp.repeat(jnp.exp(steps), extent[dim] // shards_of).reshape((-1,) + (1,) * (len(extent) - 1 - dim))
    return level


def centred(own_key, dims, deviation, limit, pieces=(), held_as=jnp.bfloat16):
    array = jax.random.normal(own_key, dims, jnp.float32) * deviation
    if len(pieces) > 0:
        array = block_levels(own_key, dims, pieces, -0.22, 0.18) * array
    return jnp.clip(array, min=-limit, max=limit).astype(held_as)


def setup_inputs(seed: int = 0) -> dict:
    streams_of = jax.random.split(jax.random.key(seed), 9)
    return {
        "queries": draw_queries(jax.random.fold_in(streams_of[8], 71), 0),
        "keys": draw_keys(jax.random.fold_in(streams_of[8], 71), 0),
        "values": centred(streams_of[2], (TOKENS, CHANNELS), 1.0, 6.0, ((0, 512),)),
        "latent": centred(streams_of[3], (TOKENS, CHANNELS), 1.0, 6.0, ((0, 512),)),
        "fresh_noise": centred(streams_of[4], (SPAN_TOK, CHANNELS), 1.0, 6.0, ((0, 8),)),
        "pool_weight": centred(streams_of[5], (POOL, HEADS), POOL ** -0.5, 1.0),
        "gate_table": centred(streams_of[6], (LEVELS, CHANNELS), 1.0, 4.0),
        "levels": place_ends(jax.random.randint(streams_of[7], (N_SPAN,), 0, LEVELS), jax.random.fold_in(streams_of[7], 1), 0, LEVELS - 1).astype(jnp.int32),
    }


def reference(queries, keys, values, latent, fresh_noise, pool_weight, gate_table, levels):
    scale = HEAD_DIM ** (-0.5)
    groups = SPAN_TOK // POOL
    layout = (N_SPAN, SPAN_TOK, HEADS, HEAD_DIM)
    query_all = queries.reshape(layout)
    key_all = keys.reshape(layout)
    value_all = values.reshape(layout)
    mixing = pool_weight.astype(jnp.float32)

    def summarize(source):
        grouped = source.reshape(N_SPAN, groups, POOL, HEADS, HEAD_DIM).astype(jnp.float32)
        pooled = jnp.einsum('cjphd,ph->cjhd', grouped, mixing).astype(jnp.bfloat16)
        return lax.optimization_barrier(pooled).astype(jnp.float32).reshape(N_SPAN * groups, HEADS, HEAD_DIM)
    key_summary = summarize(key_all)
    value_summary = summarize(value_all)
    row_owner = jnp.arange(N_SPAN * groups, dtype=jnp.int32) // groups

    def one_span(item):
        query_span, key_span, value_span, position = item
        query_f = query_span.astype(jnp.float32)
        own_scores = jnp.einsum('qhd,khd->qhk', query_f, key_span.astype(jnp.float32)) * scale
        past_scores = jnp.einsum('qhd,khd->qhk', query_f, key_summary) * scale
        past_scores = jnp.where((row_owner > position)[None, None, :], past_scores, -jnp.inf)
        scores = jnp.concatenate([own_scores, past_scores], axis=2)
        top = lax.optimization_barrier(jnp.max(scores, axis=2, keepdims=True))
        weights = jnp.exp(scores - top)
        total = lax.optimization_barrier(jnp.sum(weights, axis=2))
        rounded = lax.optimization_barrier(weights.astype(jnp.bfloat16)).astype(jnp.float32)
        stacked = jnp.concatenate([value_span.astype(jnp.float32), value_summary], axis=0)
        mixed = jnp.einsum('qhk,khd->qhd', rounded, stacked) / total[:, :, None]
        return mixed.astype(jnp.bfloat16).reshape(SPAN_TOK, CHANNELS)
    attention = lax.map(one_span, (query_all, key_all, value_all, jnp.arange(N_SPAN, dtype=jnp.int32)))
    attention = lax.optimization_barrier(attention).astype(jnp.float32)
    inverse = 1.0 / jnp.sqrt(lax.optimization_barrier(jnp.mean(attention * attention, axis=2, keepdims=True)) + 1e-06)
    gates = jnp.take(gate_table.astype(jnp.float32), levels, axis=0)
    sigma = (levels.astype(jnp.float32) + 1.0) / LEVELS
    velocity = gates[:, None, :] * attention * inverse
    cleaned = (latent.reshape(N_SPAN, SPAN_TOK, CHANNELS).astype(jnp.float32) - sigma[:, None, None] * velocity).astype(jnp.bfloat16)
    cleaned = cleaned.reshape(TOKENS, CHANNELS)
    return jnp.concatenate([fresh_noise, cleaned[:TOKENS - SPAN_TOK]], axis=0)
```

```python
import functools
import math

import jax
import jax.numpy as jnp
from jax import lax
from jax.experimental import pallas as pl
from jax.experimental.pallas import tpu as pltpu
from jax.sharding import PartitionSpec as P

HEAD_DIM = 128
POOL = 32
CHUNKS = 4
NX = 4
MESH = pl.DeviceIdType.MESH
F32 = jnp.float32
BF16 = jnp.bfloat16


def kernel(
    nz, nx, ns, heads,
    q_ref, k_ref, v_ref, lat_ref, fresh_ref, pool_ref, gate_ref, lev_ref, out_ref,
    qbuf, kbuf, vbuf, sum_send, sum_recv, sbuf, m_buf, acc_buf, obuf, att, lat, cbuf, shift, coef,
    qkv_s, qkv_r, loc, ss, sr, xs, xr, ds_, dr, us, ur, os_, or_, hs_, hr, fin,
):
    nsp = nz * nx
    hl = heads // ns
    width = hl * HEAD_DIM
    tl = k_ref.shape[0]
    rows = tl // CHUNKS
    groups = tl // POOL
    gr = groups * ns
    cs = nz // 4
    nd, nu = nz // 2, nz // 2 - 1
    qn = ns * rows
    c_exp = HEAD_DIM ** (-0.5) * math.log2(math.e)

    span = lax.axis_index("span")
    seq = lax.axis_index("seq")
    z = lax.div(span, nx)
    x = lax.rem(span, nx)
    zdn = lax.rem(z + nz - 1, nz) * nx + x
    zup = lax.rem(z + 1, nz) * nx + x
    nxt = lax.rem(span + 1, nsp)
    prv = lax.rem(span + nsp - 1, nsp)

    def peer(o):
        return lax.rem(seq + o, ns)

    def source(o):
        return lax.rem(seq + ns - o, ns)

    def head_cols(s):
        return pl.ds(pl.multiple_of(s * width, HEAD_DIM), width)

    def remote(src, dst, send, recv, s, q):
        return pltpu.make_async_remote_copy(
            src_ref=src, dst_ref=dst, send_sem=send, recv_sem=recv, device_id=(s, q), device_id_type=MESH
        )

    def clear(i, carry):
        for part in range(2):
            sbuf[part, i] = jnp.zeros(sbuf.shape[2:], BF16)
        return carry

    lax.fori_loop(0, nz, clear, 0)

    barrier = pltpu.get_barrier_semaphore()

    def greet(s, q):
        pl.semaphore_signal(barrier, inc=1, device_id=(s, q), device_id_type=MESH)

    for o in range(1, ns):
        greet(span, peer(o))
    for o in range(1, nx):
        greet(z * nx + lax.rem(x + o, nx), seq)
    for s in (zdn, zup, nxt, prv):
        greet(s, seq)

    lat_copy = pltpu.make_async_copy(lat_ref, lat, loc.at[4])
    lat_copy.start()
    fresh_copy = pltpu.make_async_copy(fresh_ref, shift, loc.at[5])

    @pl.when(span == 0)
    def _():
        fresh_copy.start()

    pl.semaphore_wait(barrier, ns - 1 + nx - 1 + 4)

    def qkv_copy(t, o):
        d = peer(o)
        if t == 1:
            src, dst = q_ref.at[:, :, head_cols(d)], qbuf.at[:, seq]
        else:
            src, dst = (k_ref, v_ref)[t // 2].at[:, head_cols(d)], (kbuf, vbuf)[t // 2].at[seq]
        return remote(src, dst, qkv_s.at[t, o], qkv_r.at[t, o], span, d)

    def qkv_arrival(t, o):
        s = source(o)
        if t == 1:
            dst = qbuf.at[:, s]
        else:
            dst = (kbuf, vbuf)[t // 2].at[s]
        return pltpu.make_async_copy(dst, dst, qkv_r.at[t, o])

    own = (
        pltpu.make_async_copy(k_ref.at[:, head_cols(seq)], kbuf.at[seq], loc.at[0]),
        pltpu.make_async_copy(q_ref.at[:, :, head_cols(seq)], qbuf.at[:, seq], loc.at[1]),
        pltpu.make_async_copy(v_ref.at[:, head_cols(seq)], vbuf.at[seq], loc.at[2]),
    )

    for h in range(heads):
        cols = slice(h * HEAD_DIM, (h + 1) * HEAD_DIM)
        w = jnp.broadcast_to(pool_ref[:, h : h + 1].astype(F32), (POOL, HEAD_DIM))
        parts = []
        for ref in (k_ref, v_ref):
            grouped = ref[:, cols].astype(F32).reshape(groups, POOL, HEAD_DIM)
            parts.append(jnp.sum(grouped * w[None], axis=1))
        block = jnp.concatenate(parts, axis=0).astype(BF16)
        sum_send[h // hl, :, (h % hl) * HEAD_DIM : (h % hl + 1) * HEAD_DIM] = block

    def sum_copy(o):
        return remote(sum_send.at[peer(o)], sum_recv.at[seq], ss.at[o], sr.at[o], span, peer(o))

    def sum_arrival(o):
        dst = sum_recv.at[source(o)]
        return pltpu.make_async_copy(dst, dst, sr.at[o])

    own_sum = pltpu.make_async_copy(sum_send.at[seq], sum_recv.at[seq], loc.at[3])
    own_sum.start()
    for o in range(1, ns):
        sum_copy(o).start()
    for t in range(3):
        own[t].start()
        for o in range(1, ns):
            qkv_copy(t, o).start()

    level = lev_ref[0]
    sigma = (level.astype(F32) + 1.0) / gate_ref.shape[0]
    row_id = lax.broadcasted_iota(jnp.int32, gate_ref.shape, 0)
    row = jnp.sum(jnp.where(row_id == level, gate_ref[...].astype(F32), 0.0), axis=0, keepdims=True)
    coef[...] = jnp.broadcast_to(row * sigma, coef.shape)

    own_sum.wait()
    for o in range(1, ns):
        sum_arrival(o).wait()
    stacked = sum_recv[...].reshape(ns * 2 * groups, width)
    to_row = lax.broadcasted_iota(jnp.int32, (2 * gr, 2 * gr), 0)
    from_row = lax.broadcasted_iota(jnp.int32, (2 * gr, 2 * gr), 1)
    is_value = (to_row >= gr).astype(jnp.int32)
    within = to_row - is_value * gr
    wanted = (within // groups) * (2 * groups) + is_value * groups + within % groups
    order = (from_row == wanted).astype(F32).astype(BF16)
    sorted_rows = jnp.dot(order, stacked, preferred_element_type=F32).astype(BF16)
    sbuf[0, 0, x] = sorted_rows[:gr]
    sbuf[1, 0, x] = sorted_rows[gr:]

    def x_copy(o):
        return remote(
            sbuf.at[:, 0, x], sbuf.at[:, 0, x], xs.at[o], xr.at[o], z * nx + lax.rem(x + o, nx), seq
        )

    def x_arrival(o):
        dst = sbuf.at[:, 0, lax.rem(x + nx - o, nx)]
        return pltpu.make_async_copy(dst, dst, xr.at[o])

    for o in range(1, nx):
        x_copy(o).start()

    def down_copy(k, part):
        return remote(
            sbuf.at[part, k - 1], sbuf.at[part, k], ds_.at[k, part], dr.at[k, part], zdn, seq
        )

    def up_copy(k, part):
        return remote(
            sbuf.at[part, (nz + 1 - k) % nz], sbuf.at[part, nz - k], us.at[k, part], ur.at[k, part], zup, seq
        )

    def down_sends(k):
        return jnp.logical_and(z >= 1, z + k <= nz)

    def up_sends(k):
        return lax.rem(z - k + 1 + nz, nz) >= nz - nu

    def arrival(sem, slot, part):
        dst = sbuf.at[part, slot]
        return pltpu.make_async_copy(dst, dst, sem)

    for o in range(1, nx):
        x_arrival(o).wait()
    for part in range(2):

        @pl.when(down_sends(1))
        def _():
            down_copy(1, part).start()

        @pl.when(up_sends(1))
        def _():
            up_copy(1, part).start()

    def relay(k):
        for part in range(2):

            @pl.when(z + k <= nz - 1)
            def _():
                arrival(dr.at[k, part], k, part).wait()
                if k < nd:

                    @pl.when(z >= 1)
                    def _():
                        down_copy(k + 1, part).start()

            if k <= nu:

                @pl.when(lax.rem(z - k + nz, nz) >= nz - nu)
                def _():
                    arrival(ur.at[k, part], nz - k, part).wait()
                    if k < nu:
                        up_copy(k + 1, part).start()

    def head_slice(h):
        return slice(h * HEAD_DIM, (h + 1) * HEAD_DIM)

    def with_ones(v):
        return jnp.concatenate([v, jnp.ones(v.shape, v.dtype)], axis=1)

    def score(h, j, k):
        q = qbuf[j, :, :, head_slice(h)].reshape(qn, HEAD_DIM)
        return lax.dot_general(q, k, (((1,), (1,)), ((), ())), preferred_element_type=F32)

    def own_step(h, j):
        s = score(h, j, kbuf[:, :, head_slice(h)].reshape(ns * tl, HEAD_DIM))
        top = jnp.max(s, axis=1, keepdims=True)
        p = jnp.exp2((s - top) * c_exp).astype(BF16)
        v = with_ones(vbuf[:, :, head_slice(h)].reshape(ns * tl, HEAD_DIM))
        acc_buf[h, j] = jnp.dot(p, v, preferred_element_type=F32)
        m_buf[h, j] = jnp.broadcast_to(top, (qn, HEAD_DIM))

    def past_step(h, j, chunk):
        count = cs * nx * gr
        slots = pl.ds(chunk * cs, cs)
        s = score(h, j, sbuf[0, slots, :, :, head_slice(h)].reshape(count, HEAD_DIM))
        at = lax.broadcasted_iota(jnp.int32, (1, count), 1)
        ahead = chunk * cs * nx + at // gr
        valid = jnp.logical_and(ahead > x, z * nx + ahead < nsp)
        s = s + jnp.where(valid, 0.0, -1e30)
        before = m_buf[h, j][:, :1]
        top = jnp.maximum(before, jnp.max(s, axis=1, keepdims=True))
        p = jnp.exp2((s - top) * c_exp).astype(BF16)
        factor = jnp.exp2((before - top) * c_exp)
        v = with_ones(sbuf[1, slots, :, :, head_slice(h)].reshape(count, HEAD_DIM))
        acc_buf[h, j] = acc_buf[h, j] * factor + jnp.dot(p, v, preferred_element_type=F32)
        m_buf[h, j] = jnp.broadcast_to(top, (qn, HEAD_DIM))

    def first_pass(h):
        def step(j, carry):
            own_step(h, j)
            past_step(h, j, 0)

            @pl.when(z + 3 * cs <= nz - 1)
            def _():
                past_step(h, j, 3)

            return carry

        lax.fori_loop(0, CHUNKS, step, 0)

    last_relay = nd
    early = max(1, min(nd, cs + 1))
    for k in range(1, early + 1):
        relay(k)
    for t in range(3):
        own[t].wait()
        for o in range(1, ns):
            qkv_arrival(t, o).wait()
    for h in range(hl):
        first_pass(h)
        if early + 1 + h <= nd:
            relay(early + 1 + h)
    for k in range(early + 1 + hl, last_relay + 1):
        relay(k)

    def out_copy(j, o):
        return remote(obuf.at[j, peer(o)], att.at[j, seq], os_.at[j, o], or_.at[j, o], span, peer(o))

    def out_arrival(j, o):
        dst = att.at[j, source(o)]
        return pltpu.make_async_copy(dst, dst, or_.at[j, o])

    def own_out(j):
        return pltpu.make_async_copy(obuf.at[j, seq], att.at[j, seq], os_.at[j, 0])

    def shift_copy(j):
        return remote(cbuf.at[j], shift.at[j], hs_.at[j], hr.at[j], nxt, seq)

    def shift_arrival(j):
        return pltpu.make_async_copy(shift.at[j], shift.at[j], hr.at[j])

    lat_copy.wait()

    def second_pass(j):
        for h in range(hl):
            for chunk in (1, 2):

                @pl.when(z + chunk * cs <= nz - 1)
                def _():
                    past_step(h, j, chunk)

            acc = acc_buf[h, j]
            o = (acc[:, :HEAD_DIM] / acc[:, HEAD_DIM:]).astype(BF16)
            obuf[j, :, :, head_slice(h)] = o.reshape(ns, rows, HEAD_DIM)
        own_out(j).start()
        for o in range(1, ns):
            out_copy(j, o).start()

    def finish(j):
        own_out(j).wait()
        for o in range(1, ns):
            out_arrival(j, o).wait()
        square = jnp.zeros((rows, HEAD_DIM), F32)
        for s in range(ns):
            for h in range(hl):
                a = att[j, s, :, head_slice(h)].astype(F32)
                square = square + a * a
        mean = jnp.sum(square, axis=1, keepdims=True) / (heads * HEAD_DIM)
        inverse = jnp.broadcast_to(lax.rsqrt(mean + 1e-06), (rows, HEAD_DIM))
        for s in range(ns):
            for h in range(hl):
                cols = slice((s * hl + h) * HEAD_DIM, (s * hl + h + 1) * HEAD_DIM)
                a = att[j, s, :, head_slice(h)].astype(F32)
                cleaned = lat[j, :, cols].astype(F32) - coef[:1, cols] * a * inverse
                cbuf[j, :, cols] = cleaned.astype(BF16)

        @pl.when(span < nsp - 1)
        def _():
            shift_copy(j).start()

    def tail(j, carry):
        @pl.when(j < CHUNKS)
        def _():
            second_pass(j)

        @pl.when(j >= 1)
        def _():
            finish(j - 1)

        return carry

    lax.fori_loop(0, CHUNKS + 1, tail, 0)

    @pl.when(span == 0)
    def _():
        fresh_copy.wait()

    def leave(j):
        return pltpu.make_async_copy(shift.at[j], out_ref.at[j], fin.at[j])

    for j in range(CHUNKS):

        @pl.when(span > 0)
        def _():
            shift_arrival(j).wait()

        leave(j).start()

    for t in range(3):
        for o in range(1, ns):
            qkv_copy(t, o).wait_send()
    for o in range(1, ns):
        sum_copy(o).wait_send()
    for o in range(1, nx):
        x_copy(o).wait_send()
    for part in range(2):
        for k in range(1, nd + 1):

            @pl.when(down_sends(k))
            def _():
                down_copy(k, part).wait_send()

        for k in range(1, nu + 1):

            @pl.when(up_sends(k))
            def _():
                up_copy(k, part).wait_send()

    for j in range(CHUNKS):
        for o in range(1, ns):
            out_copy(j, o).wait_send()

        @pl.when(span < nsp - 1)
        def _():
            shift_copy(j).wait_send()

        leave(j).wait()


def local(nz, nx, queries, keys, values, latent, fresh_noise, pool_weight, gate_table, levels):
    ns = lax.axis_size("seq")
    tl, channels = keys.shape
    heads = channels // HEAD_DIM
    hl = heads // ns
    width = hl * HEAD_DIM
    rows = tl // CHUNKS
    groups = tl // POOL
    gr = groups * ns
    qn = ns * rows
    nd = nz // 2
    split = (CHUNKS, rows, channels)
    vmem = pl.BlockSpec(memory_space=pltpu.VMEM)
    far = pl.BlockSpec(memory_space=pl.ANY)
    dma = pltpu.SemaphoreType.DMA
    out = pl.pallas_call(
        functools.partial(kernel, nz, nx, ns, heads),
        out_shape=jax.ShapeDtypeStruct(split, BF16),
        in_specs=[far, vmem, vmem, far, far, vmem, vmem, pl.BlockSpec(memory_space=pltpu.SMEM)],
        out_specs=far,
        scratch_shapes=[
            pltpu.VMEM((CHUNKS, ns, rows, width), BF16),
            pltpu.VMEM((ns, tl, width), BF16),
            pltpu.VMEM((ns, tl, width), BF16),
            pltpu.VMEM((ns, 2 * groups, width), BF16),
            pltpu.VMEM((ns, 2 * groups, width), BF16),
            pltpu.VMEM((2, nz, nx, gr, width), BF16),
            pltpu.VMEM((hl, CHUNKS, qn, HEAD_DIM), F32),
            pltpu.VMEM((hl, CHUNKS, qn, 2 * HEAD_DIM), F32),
            pltpu.VMEM((CHUNKS, ns, rows, width), BF16),
            pltpu.VMEM((CHUNKS, ns, rows, width), BF16),
            pltpu.VMEM(split, BF16),
            pltpu.VMEM(split, BF16),
            pltpu.VMEM(split, BF16),
            pltpu.VMEM((8, channels), F32),
            dma((3, ns)),
            dma((3, ns)),
            dma((6,)),
            dma((ns,)),
            dma((ns,)),
            dma((nx,)),
            dma((nx,)),
            dma((nd + 1, 2)),
            dma((nd + 1, 2)),
            dma((nd + 1, 2)),
            dma((nd + 1, 2)),
            dma((CHUNKS, ns)),
            dma((CHUNKS, ns)),
            dma((CHUNKS,)),
            dma((CHUNKS,)),
            dma((CHUNKS,)),
        ],
        compiler_params=pltpu.CompilerParams(
            collective_id=0, has_side_effects=True, vmem_limit_bytes=60 * 1024 * 1024
        ),
        name="step",
    )(
        queries.reshape(split),
        keys,
        values,
        latent.reshape(split),
        fresh_noise.reshape(split),
        pool_weight,
        gate_table,
        levels,
    )
    return out.reshape(tl, channels)


def solution(mesh, nx=NX):
    placed = (
        P(("span", "seq"), None),
        P(("span", "seq"), None),
        P(("span", "seq"), None),
        P(("span", "seq"), None),
        P("seq", None),
        P(),
        P(),
        P("span"),
    )
    return jax.shard_map(
        functools.partial(local, mesh.shape["span"] // nx, nx),
        mesh=mesh,
        in_specs=placed,
        out_specs=P(("span", "seq"), None),
        check_vma=False,
    )
```

```python
import functools
import math

import jax
import jax.numpy as jnp
from jax import lax
from jax.experimental import pallas as pl
from jax.experimental.pallas import tpu as pltpu
from jax.sharding import PartitionSpec as P

HEAD_DIM = 128
POOL = 32
CHUNKS = 4
NX = 4
VMEM_LIMIT = 60 * 1024 * 1024
MESH = pl.DeviceIdType.MESH
F32 = jnp.float32
BF16 = jnp.bfloat16


def kernel(
    nz, nx, ns, heads,
    q_ref, k_ref, v_ref, lat_ref, pool_ref, gate_ref, lev_ref, out_ref,
    kin, vin, gin, qbuf, kbuf, vbuf, sum_send, sum_recv, sk, sv, m_buf, l_buf, acc_buf, obuf, att, lat, cbuf, coef,
    qkv_s, qkv_r, loc, ss, sr, kxs, kxr, kds, kdr, kus, kur, vds, vdr, vus, vur, vxs, vxr, os_, or_, hs_, hr,
):
    nsp = nz * nx
    hl = heads // ns
    tl = kin.shape[0]
    rows = tl // CHUNKS
    groups = tl // POOL
    gr = groups * ns
    plane = nx * gr
    width = hl * HEAD_DIM
    cs = nz // 4
    nd, nu = nz // 2, nz // 2 - 1
    qn = ns * rows
    c_exp = HEAD_DIM ** (-0.5) * math.log2(math.e)

    span = lax.axis_index("span")
    seq = lax.axis_index("seq")
    z = lax.div(span, nx)
    x = lax.rem(span, nx)
    zdn = lax.rem(z + nz - 1, nz) * nx + x
    zup = lax.rem(z + 1, nz) * nx + x
    nxt = lax.rem(span + 1, nsp)
    prv = lax.rem(span + nsp - 1, nsp)
    far_first = sorted(range(1, ns), key=lambda o: abs(o - ns // 2))
    sides = sorted(range(1, nx), key=lambda d: min(d, nx - d))

    def peer(o):
        return lax.rem(seq + o, ns)

    def source(o):
        return lax.rem(seq + ns - o, ns)

    def x_span(dx):
        return z * nx + lax.rem(x + dx, nx)

    def x_source(dx):
        return lax.rem(x + nx - dx, nx)

    def head_cols(s, h):
        return pl.ds(pl.multiple_of((s * hl + h) * HEAD_DIM, HEAD_DIM), HEAD_DIM)

    def remote(src, dst, send, recv, s, q):
        return pltpu.make_async_remote_copy(
            src_ref=src, dst_ref=dst, send_sem=send, recv_sem=recv, device_id=(s, q), device_id_type=MESH
        )

    def landed(dst, sem):
        return pltpu.make_async_copy(dst, dst, sem)

    def load(i, src, dst):
        return pltpu.make_async_copy(src, dst, loc.at[i])

    loads = [load(0, k_ref, kin), load(1, v_ref, vin), load(2, gate_ref, gin), load(3, lat_ref, lat)]
    for c in loads:
        c.start()

    barrier = pltpu.get_barrier_semaphore()

    def greet(s, q):
        pl.semaphore_signal(barrier, inc=1, device_id=(s, q), device_id_type=MESH)

    for o in far_first:
        greet(span, peer(o))
    for s in (prv, zdn, zup):
        greet(s, seq)
    for dx in reversed(sides):
        greet(x_span(dx), seq)

    eye = lax.broadcasted_iota(jnp.int32, (POOL, POOL), 0) == lax.broadcasted_iota(jnp.int32, (POOL, POOL), 1)
    mixing = lax.dot_general(
        eye.astype(F32).astype(BF16), pool_ref[...], (((1,), (1,)), ((), ())), preferred_element_type=F32
    )
    loads[0].wait()
    loads[1].wait()
    for h in range(heads):
        cols = slice(h * HEAD_DIM, (h + 1) * HEAD_DIM)
        w = jnp.broadcast_to(mixing[:, h : h + 1], (POOL, HEAD_DIM))
        parts = []
        for ref in (kin, vin):
            grouped = ref[:, cols].astype(F32).reshape(groups, POOL, HEAD_DIM)
            parts.append(jnp.sum(grouped * w[None], axis=1))
        block = jnp.concatenate(parts, axis=0).astype(BF16)
        sum_send[h // hl, :, (h % hl) * HEAD_DIM : (h % hl + 1) * HEAD_DIM] = block

    pl.semaphore_wait(barrier, ns - 1 + 3 + nx - 1)

    def sum_copy(o):
        return remote(sum_send.at[peer(o)], sum_recv.at[seq], ss.at[o], sr.at[o], span, peer(o))

    own_sum = pltpu.make_async_copy(sum_send.at[seq], sum_recv.at[seq], ss.at[0])
    own_sum.start()
    for o in far_first:
        sum_copy(o).start()

    def qkv_copy(h, t, o):
        d = peer(o)
        if t == 1:
            src, dst = q_ref.at[:, :, head_cols(d, h)], qbuf.at[h, :, seq]
        else:
            src, dst = (k_ref, v_ref)[t // 2].at[:, head_cols(d, h)], (kbuf, vbuf)[t // 2].at[h, seq]
        i = h * 3 + t
        if o == 0:
            return pltpu.make_async_copy(src, dst, qkv_s.at[i, 0])
        return remote(src, dst, qkv_s.at[i, o], qkv_r.at[i, o], span, d)

    def qkv_arrival(h, t, o):
        s = source(o)
        dst = qbuf.at[h, :, s] if t == 1 else (kbuf, vbuf)[t // 2].at[h, s]
        return landed(dst, qkv_r.at[h * 3 + t, o])

    for h in range(hl):
        for t in range(3):
            for o in range(ns):
                qkv_copy(h, t, o).start()

    def qkv_wait(h):
        for t in range(3):
            qkv_copy(h, t, 0).wait()
            for o in range(1, ns):
                qkv_arrival(h, t, o).wait()

    to_row = lax.broadcasted_iota(jnp.int32, (2 * gr, 2 * gr), 0)
    from_row = lax.broadcasted_iota(jnp.int32, (2 * gr, 2 * gr), 1)
    is_value = (to_row >= gr).astype(jnp.int32)
    within = to_row - is_value * gr
    wanted = (within // groups) * (2 * groups) + is_value * groups + within % groups
    order = (from_row == wanted).astype(F32).astype(BF16)

    own_sum.wait()
    for o in reversed(far_first):
        landed(sum_recv.at[source(o)], sr.at[o]).wait()
    stacked = sum_recv[...].reshape(2 * gr, width)
    sorted_rows = jnp.dot(order, stacked, preferred_element_type=F32).astype(BF16)
    sk[0, x] = sorted_rows[:gr]
    sv[0, x] = sorted_rows[gr:]

    def k_down(k, i):
        return remote(sk.at[k - 1, i], sk.at[k, i], kds.at[k, i], kdr.at[k, i], zdn, seq)

    def k_up(k, i):
        return remote(sk.at[(nz + 1 - k) % nz, i], sk.at[nz - k, i], kus.at[k, i], kur.at[k, i], zup, seq)

    def v_down(k):
        return remote(sv.at[k - 1, x], sv.at[k, x], vds.at[k], vdr.at[k], zdn, seq)

    def v_up(k):
        return remote(sv.at[(nz + 1 - k) % nz, x], sv.at[nz - k, x], vus.at[k], vur.at[k], zup, seq)

    def v_side(slot, dx):
        return remote(sv.at[slot, x], sv.at[slot, x], vxs.at[slot, dx], vxr.at[slot, dx], x_span(dx), seq)

    def k_side(dx):
        return remote(sk.at[0, x], sk.at[0, x], kxs.at[dx], kxr.at[dx], x_span(dx), seq)

    def down_sends(k):
        return jnp.logical_and(z >= 1, z + k <= nz)

    def up_sends(k):
        return lax.rem(z - k + 1 + nz, nz) >= nz - nu

    def first_keys(i):
        @pl.when(down_sends(1))
        def _():
            k_down(1, i).start()

        @pl.when(up_sends(1))
        def _():
            k_up(1, i).start()

    for dx in sides:
        k_side(dx).start()

    @pl.when(down_sends(1))
    def _():
        v_down(1).start()

    @pl.when(up_sends(1))
    def _():
        v_up(1).start()

    first_keys(x)
    for dx in sides:
        v_side(0, dx).start()

    def blank(slot):
        sk[slot] = jnp.zeros(sk.shape[1:], BF16)
        sv[slot] = jnp.zeros(sv.shape[1:], BF16)

    for slot in range(1, nz):
        if slot <= nd:

            @pl.when(z + slot >= nz)
            def _():
                blank(slot)

        else:
            passes = up_sends(nz - slot + 1)

            @pl.when(jnp.logical_not(passes))
            def _():
                blank(slot)

            @pl.when(jnp.logical_and(passes, z + slot >= nz))
            def _():
                for dx in range(1, nx):
                    sv[slot, x_source(dx)] = jnp.zeros(sv.shape[2:], BF16)

    for dx in sides:
        landed(sk.at[0, x_source(dx)], kxr.at[dx]).wait()
        first_keys(x_source(dx))

    loads[2].wait()
    level = lev_ref[0]
    sigma = (level.astype(F32) + 1.0) / gin.shape[0]
    row_id = lax.broadcasted_iota(jnp.int32, gin.shape, 0)
    row = jnp.sum(jnp.where(row_id == level, gin[...].astype(F32), 0.0), axis=0, keepdims=True)
    coef[...] = jnp.broadcast_to(row * sigma, coef.shape)

    def relay_values(k):
        @pl.when(z + k <= nz - 1)
        def _():
            landed(sv.at[k, x], vdr.at[k]).wait()
            if k < nd:

                @pl.when(z >= 1)
                def _():
                    v_down(k + 1).start()

            for dx in range(1, nx):
                v_side(k, dx).start()

        if k <= nu:

            @pl.when(up_sends(k + 1))
            def _():
                landed(sv.at[nz - k, x], vur.at[k]).wait()
                if k < nu:
                    v_up(k + 1).start()

                @pl.when(k >= z + 1)
                def _():
                    for dx in range(1, nx):
                        v_side(nz - k, dx).start()

    def relay_keys(k, i):
        @pl.when(z + k <= nz - 1)
        def _():
            landed(sk.at[k, i], kdr.at[k, i]).wait()
            if k < nd:

                @pl.when(z >= 1)
                def _():
                    k_down(k + 1, i).start()

        if k <= nu:

            @pl.when(up_sends(k + 1))
            def _():
                landed(sk.at[nz - k, i], kur.at[k, i]).wait()
                if k < nu:
                    k_up(k + 1, i).start()

    def sides_ready(chunk):
        for slot in range(chunk * cs, (chunk + 1) * cs):

            @pl.when(z + slot <= nz - 1)
            def _():
                for dx in range(1, nx):
                    landed(sv.at[slot, x_source(dx)], vxr.at[slot, dx]).wait()

    def head_slice(h):
        return slice(h * HEAD_DIM, (h + 1) * HEAD_DIM)

    def score(h, j, k):
        q = qbuf[h, j].reshape(qn, HEAD_DIM)
        return lax.dot_general(q, k, (((1,), (1,)), ((), ())), preferred_element_type=F32)

    def own_step(h, j):
        s = score(h, j, kbuf[h].reshape(ns * tl, HEAD_DIM))
        top = jnp.max(s, axis=1, keepdims=True)
        p = jnp.exp2((s - top) * c_exp)
        l_buf[h, j] = jnp.broadcast_to(jnp.sum(p, axis=1, keepdims=True), (qn, HEAD_DIM))
        v = vbuf[h].reshape(ns * tl, HEAD_DIM)
        acc_buf[h, j] = jnp.dot(p.astype(BF16), v, preferred_element_type=F32)
        m_buf[h, j] = jnp.broadcast_to(top, (qn, HEAD_DIM))

    def past_step(h, j):
        count = nz * plane
        s = score(h, j, sk[:, :, :, head_slice(h)].reshape(count, HEAD_DIM))
        ahead = lax.broadcasted_iota(jnp.int32, (1, count), 1) // gr
        valid = jnp.logical_and(ahead > x, z * nx + ahead < nsp)
        s = s + jnp.where(valid, 0.0, -1e30)
        before = m_buf[h, j]
        top = jnp.maximum(before, jnp.max(s, axis=1, keepdims=True))
        p = jnp.exp2((s - top[:, :1]) * c_exp)
        factor = jnp.exp2((before - top) * c_exp)
        total = l_buf[h, j] * factor + jnp.sum(p, axis=1, keepdims=True)
        v = sv[:, :, :, head_slice(h)].reshape(count, HEAD_DIM)
        mixed = acc_buf[h, j] * factor + jnp.dot(p.astype(BF16), v, preferred_element_type=F32)
        o = (mixed / total).astype(BF16)
        obuf[j, h] = o.reshape(ns, rows, HEAD_DIM)

    def own_work(h):
        def run(pair):
            own_step(h, 2 * pair)
            own_step(h, 2 * pair + 1)

        return run

    def hop(k, work):
        relay_values(k)
        if work is None:
            for d in [0] + sides:
                relay_keys(k, x_source(d))
            return

        def step(pair, carry):
            for i in range(nx // 2):
                d = pair * (nx // 2) + i
                relay_keys(k, x_source(d))
            work(pair)
            return carry

        lax.fori_loop(0, CHUNKS // 2, step, 0)

    work_at = {2: 0, 5: 1} if nd == 8 else {}
    for k in range(1, nd + 1):
        if k in work_at:
            qkv_wait(work_at[k])
            hop(k, own_work(work_at[k]))
        else:
            hop(k, None)
    for h in range(hl):
        if h not in work_at.values():
            qkv_wait(h)
            own_work(h)(0)
            own_work(h)(1)
    for c in range(4):
        sides_ready(c)

    def out_copy(j, h, o):
        sems = os_.at[j, h, o], or_.at[j, h, o]
        return remote(obuf.at[j, h, peer(o)], att.at[j, h, seq], *sems, span, peer(o))

    def own_out(j, h):
        return pltpu.make_async_copy(obuf.at[j, h, seq], att.at[j, h, seq], os_.at[j, h, 0])

    def shift_copy(j):
        return remote(cbuf.at[j], out_ref.at[j], hs_.at[j], hr.at[j], nxt, seq)

    loads[3].wait()

    def second_pass(j):
        for h in range(hl):
            past_step(h, j)
            for o in far_first:
                out_copy(j, h, o).start()
            own_out(j, h).start()

    def finish(j):
        for h in range(hl):
            own_out(j, h).wait()
            for o in range(1, ns):
                landed(att.at[j, h, source(o)], or_.at[j, h, o]).wait()
        square = jnp.zeros((rows, HEAD_DIM), F32)
        for s in range(ns):
            for h in range(hl):
                a = att[j, h, s].astype(F32)
                square = square + a * a
        mean = jnp.sum(square, axis=1, keepdims=True) / (heads * HEAD_DIM)
        inverse = jnp.broadcast_to(lax.rsqrt(mean + 1e-06), (rows, HEAD_DIM))
        for s in range(ns):
            for h in range(hl):
                cols = slice((s * hl + h) * HEAD_DIM, (s * hl + h + 1) * HEAD_DIM)
                a = att[j, h, s].astype(F32)
                cleaned = lat[j, :, cols].astype(F32) - coef[:1, cols] * a * inverse
                cbuf[j, :, cols] = cleaned.astype(BF16)

        @pl.when(span < nsp - 1)
        def _():
            shift_copy(j).start()

    def tail(j, carry):
        @pl.when(j < CHUNKS)
        def _():
            second_pass(j)

        @pl.when(j >= 1)
        def _():
            finish(j - 1)

        return carry

    lax.fori_loop(0, CHUNKS + 1, tail, 0)

    @pl.when(span > 0)
    def _():
        for j in range(CHUNKS):
            landed(out_ref.at[j], hr.at[j]).wait()

    for h in range(hl):
        for t in range(3):
            for o in range(1, ns):
                qkv_copy(h, t, o).wait_send()
    for o in range(1, ns):
        sum_copy(o).wait_send()
    for dx in range(1, nx):
        k_side(dx).wait_send()
    for k in range(1, nd + 1):

        @pl.when(down_sends(k))
        def _():
            v_down(k).wait_send()
            for i in range(nx):
                k_down(k, i).wait_send()

    for k in range(1, nu + 1):

        @pl.when(up_sends(k))
        def _():
            v_up(k).wait_send()
            for i in range(nx):
                k_up(k, i).wait_send()

    for slot in range(nz):

        @pl.when(z + slot <= nz - 1)
        def _():
            for dx in range(1, nx):
                v_side(slot, dx).wait_send()

    for j in range(CHUNKS):
        for h in range(hl):
            for o in range(1, ns):
                out_copy(j, h, o).wait_send()

        @pl.when(span < nsp - 1)
        def _():
            shift_copy(j).wait_send()


def local(nz, nx, queries, keys, values, latent, fresh_noise, pool_weight, gate_table, levels):
    ns = lax.axis_size("seq")
    tl, channels = keys.shape
    heads = channels // HEAD_DIM
    hl = heads // ns
    width = hl * HEAD_DIM
    rows = tl // CHUNKS
    groups = tl // POOL
    gr = groups * ns
    qn = ns * rows
    nd = nz // 2
    split = (CHUNKS, rows, channels)
    vmem = pl.BlockSpec(memory_space=pltpu.VMEM)
    far = pl.BlockSpec(memory_space=pl.ANY)
    dma = pltpu.SemaphoreType.DMA
    out = pl.pallas_call(
        functools.partial(kernel, nz, nx, ns, heads),
        out_shape=jax.ShapeDtypeStruct(split, BF16),
        in_specs=[far, far, far, far, vmem, far, pl.BlockSpec(memory_space=pltpu.SMEM)],
        out_specs=far,
        scratch_shapes=[
            pltpu.VMEM((tl, channels), BF16),
            pltpu.VMEM((tl, channels), BF16),
            pltpu.VMEM(gate_table.shape, BF16),
            pltpu.VMEM((hl, CHUNKS, ns, rows, HEAD_DIM), BF16),
            pltpu.VMEM((hl, ns, tl, HEAD_DIM), BF16),
            pltpu.VMEM((hl, ns, tl, HEAD_DIM), BF16),
            pltpu.VMEM((ns, 2 * groups, width), BF16),
            pltpu.VMEM((ns, 2 * groups, width), BF16),
            pltpu.VMEM((nz, nx, gr, width), BF16),
            pltpu.VMEM((nz, nx, gr, width), BF16),
            pltpu.VMEM((hl, CHUNKS, qn, HEAD_DIM), F32),
            pltpu.VMEM((hl, CHUNKS, qn, HEAD_DIM), F32),
            pltpu.VMEM((hl, CHUNKS, qn, HEAD_DIM), F32),
            pltpu.VMEM((CHUNKS, hl, ns, rows, HEAD_DIM), BF16),
            pltpu.VMEM((CHUNKS, hl, ns, rows, HEAD_DIM), BF16),
            pltpu.VMEM(split, BF16),
            pltpu.VMEM(split, BF16),
            pltpu.VMEM((8, channels), F32),
            dma((3 * hl, ns)),
            dma((3 * hl, ns)),
            dma((4,)),
            dma((ns,)),
            dma((ns,)),
            dma((nx,)),
            dma((nx,)),
            dma((nd + 1, nx)),
            dma((nd + 1, nx)),
            dma((nd + 1, nx)),
            dma((nd + 1, nx)),
            dma((nd + 1,)),
            dma((nd + 1,)),
            dma((nd + 1,)),
            dma((nd + 1,)),
            dma((nz, nx)),
            dma((nz, nx)),
            dma((CHUNKS, hl, ns)),
            dma((CHUNKS, hl, ns)),
            dma((CHUNKS,)),
            dma((CHUNKS,)),
        ],
        compiler_params=pltpu.CompilerParams(
            collective_id=0, has_side_effects=True, vmem_limit_bytes=VMEM_LIMIT
        ),
        name="step",
    )(
        queries.reshape(split),
        keys,
        values,
        latent.reshape(split),
        pool_weight.T,
        gate_table,
        levels,
    )
    return jnp.where(lax.axis_index("span") == 0, fresh_noise, out.reshape(tl, channels))


def solution(mesh, nx=NX):
    placed = (
        P(("span", "seq"), None),
        P(("span", "seq"), None),
        P(("span", "seq"), None),
        P(("span", "seq"), None),
        P("seq", None),
        P(),
        P(),
        P("span"),
    )
    return jax.shard_map(
        functools.partial(local, mesh.shape["span"] // nx, nx),
        mesh=mesh,
        in_specs=placed,
        out_specs=P(("span", "seq"), None),
        check_vma=False,
    )
```

```python
import functools
import math

import jax
import jax.numpy as jnp
from jax import lax
from jax.experimental import pallas as pl
from jax.experimental.pallas import tpu as pltpu
from jax.sharding import PartitionSpec as P

HEAD_DIM = 128
POOL = 32
CHUNKS = 4
NX = 4
VMEM_LIMIT = 60 * 1024 * 1024
MESH = pl.DeviceIdType.MESH
F32 = jnp.float32
BF16 = jnp.bfloat16


def kernel(
    nz, nx, ns, heads,
    q_ref, k_ref, v_ref, lat_ref, pool_ref, gate_ref, lev_ref, out_ref,
    kin, vin, gin, qbuf, kbuf, vbuf, sum_send, sum_recv, sk, sv, m_buf, l_buf, acc_buf, obuf, att, lat, cbuf, coef,
    qkv_s, qkv_r, loc, ss, sr, kxs, kxr, kds, kdr, kus, kur, vds, vdr, vus, vur, vxs, vxr, os_, or_, hs_, hr,
):
    nsp = nz * nx
    hl = heads // ns
    tl = kin.shape[0]
    rows = tl // CHUNKS
    groups = tl // POOL
    gr = groups * ns
    plane = nx * gr
    width = hl * HEAD_DIM
    cs = nz // 4
    nd, nu = nz // 2, nz // 2 - 1
    qn = ns * rows
    c_exp = HEAD_DIM ** (-0.5) * math.log2(math.e)

    span = lax.axis_index("span")
    seq = lax.axis_index("seq")
    z = lax.div(span, nx)
    x = lax.rem(span, nx)
    zdn = lax.rem(z + nz - 1, nz) * nx + x
    zup = lax.rem(z + 1, nz) * nx + x
    nxt = lax.rem(span + 1, nsp)
    prv = lax.rem(span + nsp - 1, nsp)
    far_first = sorted(range(1, ns), key=lambda o: abs(o - ns // 2))
    sides = sorted(range(1, nx), key=lambda d: min(d, nx - d))

    def peer(o):
        return lax.rem(seq + o, ns)

    def source(o):
        return lax.rem(seq + ns - o, ns)

    def x_span(dx):
        return z * nx + lax.rem(x + dx, nx)

    def x_source(dx):
        return lax.rem(x + nx - dx, nx)

    def head_cols(s, h):
        return pl.ds(pl.multiple_of((s * hl + h) * HEAD_DIM, HEAD_DIM), HEAD_DIM)

    def remote(src, dst, send, recv, s, q):
        return pltpu.make_async_remote_copy(
            src_ref=src, dst_ref=dst, send_sem=send, recv_sem=recv, device_id=(s, q), device_id_type=MESH
        )

    def landed(dst, sem):
        return pltpu.make_async_copy(dst, dst, sem)

    def load(i, src, dst):
        return pltpu.make_async_copy(src, dst, loc.at[i])

    loads = [load(0, k_ref, kin), load(1, v_ref, vin), load(2, gate_ref, gin), load(3, lat_ref, lat)]
    barrier = pltpu.get_barrier_semaphore()

    def greet(s, q):
        pl.semaphore_signal(barrier, inc=1, device_id=(s, q), device_id_type=MESH)

    for o in far_first:
        greet(span, peer(o))
    for s in (prv, zdn, zup):
        greet(s, seq)
    for dx in reversed(sides):
        greet(x_span(dx), seq)
    for c in loads:
        c.start()

    eye = lax.broadcasted_iota(jnp.int32, (POOL, POOL), 0) == lax.broadcasted_iota(jnp.int32, (POOL, POOL), 1)
    mixing = lax.dot_general(
        eye.astype(F32).astype(BF16), pool_ref[...], (((1,), (1,)), ((), ())), preferred_element_type=F32
    )
    loads[0].wait()
    loads[1].wait()
    for h in range(heads):
        cols = slice(h * HEAD_DIM, (h + 1) * HEAD_DIM)
        w = jnp.broadcast_to(mixing[:, h : h + 1], (POOL, HEAD_DIM))
        parts = []
        for ref in (kin, vin):
            grouped = ref[:, cols].astype(F32).reshape(groups, POOL, HEAD_DIM)
            parts.append(jnp.sum(grouped * w[None], axis=1))
        block = jnp.concatenate(parts, axis=0).astype(BF16)
        sum_send[h // hl, :, (h % hl) * HEAD_DIM : (h % hl + 1) * HEAD_DIM] = block

    pl.semaphore_wait(barrier, ns - 1 + 3 + nx - 1)

    def sum_copy(o):
        return remote(sum_send.at[peer(o)], sum_recv.at[seq], ss.at[o], sr.at[o], span, peer(o))

    own_sum = pltpu.make_async_copy(sum_send.at[seq], sum_recv.at[seq], ss.at[0])
    own_sum.start()
    for o in far_first:
        sum_copy(o).start()

    def qkv_copy(h, t, o):
        d = peer(o)
        if t == 1:
            src, dst = q_ref.at[:, :, head_cols(d, h)], qbuf.at[h, :, seq]
        else:
            src, dst = (k_ref, v_ref)[t // 2].at[:, head_cols(d, h)], (kbuf, vbuf)[t // 2].at[h, seq]
        i = h * 3 + t
        if o == 0:
            return pltpu.make_async_copy(src, dst, qkv_s.at[i, 0])
        return remote(src, dst, qkv_s.at[i, o], qkv_r.at[i, o], span, d)

    def qkv_arrival(h, t, o):
        s = source(o)
        dst = qbuf.at[h, :, s] if t == 1 else (kbuf, vbuf)[t // 2].at[h, s]
        return landed(dst, qkv_r.at[h * 3 + t, o])

    for h in range(hl):
        for t in range(3):
            for o in range(ns):
                qkv_copy(h, t, o).start()

    def qkv_wait(h):
        for t in range(3):
            qkv_copy(h, t, 0).wait()
            for o in range(1, ns):
                qkv_arrival(h, t, o).wait()

    to_row = lax.broadcasted_iota(jnp.int32, (2 * gr, 2 * gr), 0)
    from_row = lax.broadcasted_iota(jnp.int32, (2 * gr, 2 * gr), 1)
    is_value = (to_row >= gr).astype(jnp.int32)
    within = to_row - is_value * gr
    wanted = (within // groups) * (2 * groups) + is_value * groups + within % groups
    order = (from_row == wanted).astype(F32).astype(BF16)

    own_sum.wait()
    for o in reversed(far_first):
        landed(sum_recv.at[source(o)], sr.at[o]).wait()
    stacked = sum_recv[...].reshape(2 * gr, width)
    sorted_rows = jnp.dot(order, stacked, preferred_element_type=F32).astype(BF16)
    sk[0, x] = sorted_rows[:gr]
    sv[0, x] = sorted_rows[gr:]

    def k_down(k, i):
        return remote(sk.at[k - 1, i], sk.at[k, i], kds.at[k, i], kdr.at[k, i], zdn, seq)

    def k_up(k, i):
        return remote(sk.at[(nz + 1 - k) % nz, i], sk.at[nz - k, i], kus.at[k, i], kur.at[k, i], zup, seq)

    def v_down(k):
        return remote(sv.at[k - 1, x], sv.at[k, x], vds.at[k], vdr.at[k], zdn, seq)

    def v_up(k):
        return remote(sv.at[(nz + 1 - k) % nz, x], sv.at[nz - k, x], vus.at[k], vur.at[k], zup, seq)

    def v_side(slot, dx):
        return remote(sv.at[slot, x], sv.at[slot, x], vxs.at[slot, dx], vxr.at[slot, dx], x_span(dx), seq)

    def k_side(dx):
        return remote(sk.at[0, x], sk.at[0, x], kxs.at[dx], kxr.at[dx], x_span(dx), seq)

    def down_sends(k):
        return jnp.logical_and(z >= 1, z + k <= nz)

    def up_sends(k):
        return lax.rem(z - k + 1 + nz, nz) >= nz - nu

    def first_keys(i):
        @pl.when(down_sends(1))
        def _():
            k_down(1, i).start()

        @pl.when(up_sends(1))
        def _():
            k_up(1, i).start()

    for dx in sides:
        k_side(dx).start()

    @pl.when(down_sends(1))
    def _():
        v_down(1).start()

    @pl.when(up_sends(1))
    def _():
        v_up(1).start()

    first_keys(x)
    for dx in sides:
        v_side(0, dx).start()

    def blank(slot):
        sk[slot] = jnp.zeros(sk.shape[1:], BF16)
        sv[slot] = jnp.zeros(sv.shape[1:], BF16)

    for slot in range(1, nz):
        if slot <= nd:

            @pl.when(z + slot >= nz)
            def _():
                blank(slot)

        else:
            passes = up_sends(nz - slot + 1)

            @pl.when(jnp.logical_not(passes))
            def _():
                blank(slot)

            @pl.when(jnp.logical_and(passes, z + slot >= nz))
            def _():
                for dx in range(1, nx):
                    sv[slot, x_source(dx)] = jnp.zeros(sv.shape[2:], BF16)

    for dx in sides:
        landed(sk.at[0, x_source(dx)], kxr.at[dx]).wait()
        first_keys(x_source(dx))

    loads[2].wait()
    level = lev_ref[0]
    sigma = (level.astype(F32) + 1.0) / gin.shape[0]
    row_id = lax.broadcasted_iota(jnp.int32, gin.shape, 0)
    row = jnp.sum(jnp.where(row_id == level, gin[...].astype(F32), 0.0), axis=0, keepdims=True)
    coef[...] = jnp.broadcast_to(row * sigma, coef.shape)

    def relay_down(k):
        @pl.when(z + k <= nz - 1)
        def _():
            landed(sv.at[k, x], vdr.at[k]).wait()
            if k < nd:

                @pl.when(z >= 1)
                def _():
                    v_down(k + 1).start()

            for dx in range(1, nx):
                v_side(k, dx).start()
            for d in [0] + sides:
                i = x_source(d)
                landed(sk.at[k, i], kdr.at[k, i]).wait()
                if k < nd:

                    @pl.when(z >= 1)
                    def _():
                        k_down(k + 1, i).start()

    def relay_up(k):
        @pl.when(up_sends(k + 1))
        def _():
            landed(sv.at[nz - k, x], vur.at[k]).wait()
            if k < nu:
                v_up(k + 1).start()

            @pl.when(k >= z + 1)
            def _():
                for dx in range(1, nx):
                    v_side(nz - k, dx).start()

            for d in [0] + sides:
                i = x_source(d)
                landed(sk.at[nz - k, i], kur.at[k, i]).wait()
                if k < nu:
                    k_up(k + 1, i).start()

    def sides_ready(chunk):
        for slot in range(chunk * cs, (chunk + 1) * cs):

            @pl.when(z + slot <= nz - 1)
            def _():
                for dx in range(1, nx):
                    landed(sv.at[slot, x_source(dx)], vxr.at[slot, dx]).wait()

    def head_slice(h):
        return slice(h * HEAD_DIM, (h + 1) * HEAD_DIM)

    def score(h, j, k):
        q = qbuf[h, j].reshape(qn, HEAD_DIM)
        return lax.dot_general(q, k, (((1,), (1,)), ((), ())), preferred_element_type=F32)

    def own_step(h, j):
        s = score(h, j, kbuf[h].reshape(ns * tl, HEAD_DIM))
        top = jnp.max(s, axis=1, keepdims=True)
        p = jnp.exp2((s - top) * c_exp)
        l_buf[h, j] = jnp.broadcast_to(jnp.sum(p, axis=1, keepdims=True), (qn, HEAD_DIM))
        v = vbuf[h].reshape(ns * tl, HEAD_DIM)
        acc_buf[h, j] = jnp.dot(p.astype(BF16), v, preferred_element_type=F32)
        m_buf[h, j] = jnp.broadcast_to(top, (qn, HEAD_DIM))

    def past_step(h, j):
        count = nz * plane
        s = score(h, j, sk[:, :, :, head_slice(h)].reshape(count, HEAD_DIM))
        ahead = lax.broadcasted_iota(jnp.int32, (1, count), 1) // gr
        valid = jnp.logical_and(ahead > x, z * nx + ahead < nsp)
        s = s + jnp.where(valid, 0.0, -1e30)
        before = m_buf[h, j]
        top = jnp.maximum(before, jnp.max(s, axis=1, keepdims=True))
        p = jnp.exp2((s - top[:, :1]) * c_exp)
        factor = jnp.exp2((before - top) * c_exp)
        total = l_buf[h, j] * factor + jnp.sum(p, axis=1, keepdims=True)
        v = sv[:, :, :, head_slice(h)].reshape(count, HEAD_DIM)
        mixed = acc_buf[h, j] * factor + jnp.dot(p.astype(BF16), v, preferred_element_type=F32)
        o = (mixed / total).astype(BF16)
        obuf[j, h] = o.reshape(ns, rows, HEAD_DIM)

    def own_work(h):
        def run(pair):
            own_step(h, 2 * pair)
            own_step(h, 2 * pair + 1)

        return run

    plan = {2: (0, 0), 3: (0, 1), 5: (1, 0), 6: (1, 1), 7: (2, 0), 8: (2, 1)} if nd == 8 else {}
    for k in range(1, nd + 1):
        relay_down(k)
        if k <= nu:
            relay_up(k)
        if k in plan:
            h, pair = plan[k]
            if pair == 0:
                qkv_wait(h)
            own_work(h)(pair)
    if not plan:
        for h in range(hl):
            qkv_wait(h)
            own_work(h)(0)
            own_work(h)(1)
    for c in range(4):
        sides_ready(c)

    def out_copy(j, h, o):
        sems = os_.at[j, h, o], or_.at[j, h, o]
        return remote(obuf.at[j, h, peer(o)], att.at[j, h, seq], *sems, span, peer(o))

    def own_out(j, h):
        return pltpu.make_async_copy(obuf.at[j, h, seq], att.at[j, h, seq], os_.at[j, h, 0])

    def shift_copy(j):
        return remote(cbuf.at[j], out_ref.at[j], hs_.at[j], hr.at[j], nxt, seq)

    loads[3].wait()

    def second_pass(j):
        for h in range(hl):
            past_step(h, j)
            for o in far_first:
                out_copy(j, h, o).start()
            own_out(j, h).start()

    def finish(j):
        for h in range(hl):
            own_out(j, h).wait()
            for o in range(1, ns):
                landed(att.at[j, h, source(o)], or_.at[j, h, o]).wait()
        square = jnp.zeros((rows, HEAD_DIM), F32)
        for s in range(ns):
            for h in range(hl):
                a = att[j, h, s].astype(F32)
                square = square + a * a
        mean = jnp.sum(square, axis=1, keepdims=True) / (heads * HEAD_DIM)
        inverse = jnp.broadcast_to(lax.rsqrt(mean + 1e-06), (rows, HEAD_DIM))
        for s in range(ns):
            for h in range(hl):
                cols = slice((s * hl + h) * HEAD_DIM, (s * hl + h + 1) * HEAD_DIM)
                a = att[j, h, s].astype(F32)
                cleaned = lat[j, :, cols].astype(F32) - coef[:1, cols] * a * inverse
                cbuf[j, :, cols] = cleaned.astype(BF16)

        @pl.when(span < nsp - 1)
        def _():
            shift_copy(j).start()

    def tail(j, carry):
        @pl.when(j < CHUNKS)
        def _():
            second_pass(j)

        @pl.when(j >= 1)
        def _():
            finish(j - 1)

        return carry

    lax.fori_loop(0, CHUNKS + 1, tail, 0)

    @pl.when(span > 0)
    def _():
        for j in range(CHUNKS):
            landed(out_ref.at[j], hr.at[j]).wait()

    for h in range(hl):
        for t in range(3):
            for o in range(1, ns):
                qkv_copy(h, t, o).wait_send()
    for o in range(1, ns):
        sum_copy(o).wait_send()
    for dx in range(1, nx):
        k_side(dx).wait_send()
    for k in range(1, nd + 1):

        @pl.when(down_sends(k))
        def _():
            v_down(k).wait_send()
            for i in range(nx):
                k_down(k, i).wait_send()

    for k in range(1, nu + 1):

        @pl.when(up_sends(k))
        def _():
            v_up(k).wait_send()
            for i in range(nx):
                k_up(k, i).wait_send()

    for slot in range(nz):

        @pl.when(z + slot <= nz - 1)
        def _():
            for dx in range(1, nx):
                v_side(slot, dx).wait_send()

    for j in range(CHUNKS):
        for h in range(hl):
            for o in range(1, ns):
                out_copy(j, h, o).wait_send()

        @pl.when(span < nsp - 1)
        def _():
            shift_copy(j).wait_send()


def local(nz, nx, queries, keys, values, latent, fresh_noise, pool_weight, gate_table, levels):
    ns = lax.axis_size("seq")
    tl, channels = keys.shape
    heads = channels // HEAD_DIM
    hl = heads // ns
    width = hl * HEAD_DIM
    rows = tl // CHUNKS
    groups = tl // POOL
    gr = groups * ns
    qn = ns * rows
    nd = nz // 2
    split = (CHUNKS, rows, channels)
    vmem = pl.BlockSpec(memory_space=pltpu.VMEM)
    far = pl.BlockSpec(memory_space=pl.ANY)
    dma = pltpu.SemaphoreType.DMA
    out = pl.pallas_call(
        functools.partial(kernel, nz, nx, ns, heads),
        out_shape=jax.ShapeDtypeStruct(split, BF16),
        in_specs=[far, far, far, far, vmem, far, pl.BlockSpec(memory_space=pltpu.SMEM)],
        out_specs=far,
        scratch_shapes=[
            pltpu.VMEM((tl, channels), BF16),
            pltpu.VMEM((tl, channels), BF16),
            pltpu.VMEM(gate_table.shape, BF16),
            pltpu.VMEM((hl, CHUNKS, ns, rows, HEAD_DIM), BF16),
            pltpu.VMEM((hl, ns, tl, HEAD_DIM), BF16),
            pltpu.VMEM((hl, ns, tl, HEAD_DIM), BF16),
            pltpu.VMEM((ns, 2 * groups, width), BF16),
            pltpu.VMEM((ns, 2 * groups, width), BF16),
            pltpu.VMEM((nz, nx, gr, width), BF16),
            pltpu.VMEM((nz, nx, gr, width), BF16),
            pltpu.VMEM((hl, CHUNKS, qn, HEAD_DIM), F32),
            pltpu.VMEM((hl, CHUNKS, qn, HEAD_DIM), F32),
            pltpu.VMEM((hl, CHUNKS, qn, HEAD_DIM), F32),
            pltpu.VMEM((CHUNKS, hl, ns, rows, HEAD_DIM), BF16),
            pltpu.VMEM((CHUNKS, hl, ns, rows, HEAD_DIM), BF16),
            pltpu.VMEM(split, BF16),
            pltpu.VMEM(split, BF16),
            pltpu.VMEM((8, channels), F32),
            dma((3 * hl, ns)),
            dma((3 * hl, ns)),
            dma((4,)),
            dma((ns,)),
            dma((ns,)),
            dma((nx,)),
            dma((nx,)),
            dma((nd + 1, nx)),
            dma((nd + 1, nx)),
            dma((nd + 1, nx)),
            dma((nd + 1, nx)),
            dma((nd + 1,)),
            dma((nd + 1,)),
            dma((nd + 1,)),
            dma((nd + 1,)),
            dma((nz, nx)),
            dma((nz, nx)),
            dma((CHUNKS, hl, ns)),
            dma((CHUNKS, hl, ns)),
            dma((CHUNKS,)),
            dma((CHUNKS,)),
        ],
        compiler_params=pltpu.CompilerParams(
            collective_id=0, has_side_effects=True, vmem_limit_bytes=VMEM_LIMIT
        ),
        name="step",
    )(
        queries.reshape(split),
        keys,
        values,
        latent.reshape(split),
        pool_weight.T,
        gate_table,
        levels,
    )
    return jnp.where(lax.axis_index("span") == 0, fresh_noise, out.reshape(tl, channels))


def solution(mesh, nx=NX):
    placed = (
        P(("span", "seq"), None),
        P(("span", "seq"), None),
        P(("span", "seq"), None),
        P(("span", "seq"), None),
        P("seq", None),
        P(),
        P(),
        P("span"),
    )
    return jax.shard_map(
        functools.partial(local, mesh.shape["span"] // nx, nx),
        mesh=mesh,
        in_specs=placed,
        out_specs=P(("span", "seq"), None),
        check_vma=False,
    )
```
